32 devices in a mesh: parts: 2 (over y), aper: 4 (over z), rng: 2 (over x), sub: 2 (over core).
Axes of the slice: x: 2, y: 2, z: 4, core: 2. Of those that a mesh axis runs over, the one named last changes fastest.
Arguments:
- echoes: bfloat16 [2, 1024, 2048], P(None, ('parts', 'aper', 'sub'), 'rng'), parts along dimension 1, may hold values from -6 to 6
- chirp: bfloat16 [2, 512], replicated, may hold values from -0.1875 to 0.1875
- pulse_phase: float32 [1024, 64], P(('parts', 'aper', 'sub')), parts along dimension 0, may hold values from -3.140625 to 3.140625
- pulse_shift: int32 [1024, 64], P(('parts', 'aper', 'sub')), parts along dimension 0, may hold values from -8 to 8
- kernel_taps: int32 [2, 2, 8, 512], P(None, None, None, ('parts', 'aper', 'sub')), parts along dimension 3, may hold values from 0 to 31
- merge_shift: int32 [2, 2, 512], P(None, None, ('parts', 'aper', 'sub')), parts along dimension 2, may hold values from -8 to 8
- kernel_weights: float32 [2, 2, 2, 8, 512], P(None, None, None, None, ('parts', 'aper', 'sub')), parts along dimension 4, may hold values from -1 to 1
Outputs:
- image: bfloat16 [2, 512, 2048], P(None, ('parts', 'aper', 'sub'), 'rng'), parts along dimension 1
The draws below stay inside these ranges and needn't reach their ends.
There are 2 independent parts, one for each index of `parts`. The reference program is written for one: setup_inputs(seed, part) draws one part's arguments, and reference() takes and returns one part's arrays. A program takes and returns all parts, laid end to end along the dimension named above; an argument that names none is the same for every part. Nothing has to cross between parts.
All inputs are finite; a program needn't handle non-finite values.
Results may differ from the reference program's by a relative error of at most 0.0099.
Values may be sent and summed in bfloat16 or wider, within the bound.
No kernel may reach another device: no remote copies, remote signals or barrier semaphores. Data moves between devices by JAX's collectives and lax.ppermute only.
A program may use at most 128 MiB of HBM per device.

```python
import math
import jax
import jax.numpy as jnp
import numpy as np
from jax import lax

BINS = 2048
TAPS = 512
REACH = 8
KERNEL = 8
BEAM_DEV = 32
PULSE_SUB = 128
LEVELS = 2
BEAM_BASE = 64
BEAM_ROWS = 256
PULSES = 512
N_APER = 4


def with_ends(result, own_key, low, top_value):
    place = [jax.random.randint(jax.random.fold_in(own_key, axis), (), 0, length) for axis, length in enumerate(result.shape)]
    longest = result.shape.index(max(result.shape))
    neighbour = place[:longest] + [(place[longest] + 1) % result.shape[longest]] + place[longest + 1:]
    return result.at[tuple(place)].set(low).at[tuple(neighbour)].set(top_value)


def block_scale(key, extent, split, low, largest):
    loudness = 1.0
    for axis_at, blocks in split:
        draws = jax.random.uniform(jax.random.fold_in(jax.random.fold_in(key, 6), axis_at), (blocks,), jnp.float32, low / len(split), largest / len(split))
        loudness = loudness * jnp.repeat(jnp.exp(draws), extent[axis_at] // blocks).reshape((-1,) + (1,) * (len(extent) - 1 - axis_at))
    return loudness


def noise(rng, dims, width, reach, cuts=(), kind=jnp.bfloat16):
    factor_of = block_scale(rng, dims, cuts, -0.22, 0.18) if cuts else 1.0
    array = jax.random.normal(rng, dims, jnp.float32) * width * factor_of
    return jnp.minimum(jnp.maximum(array, -reach), reach).astype(kind)


def setup_inputs(seed: int = 0, part: int = 0) -> dict:
    streams_of = jax.random.split(jax.random.key(seed), 8)
    part_splits = jax.random.split(jax.random.fold_in(streams_of[7], part), 8)
    return {
        "echoes": noise(part_splits[0], (2, PULSES, BINS), 1.0, 6.0, ((1, 8), (2, 2))),
        "chirp": noise(streams_of[1], (2, TAPS), (2 * TAPS) ** -0.5, 0.1875),
        "pulse_phase": jnp.clip(jax.random.uniform(part_splits[2], (PULSES, BEAM_BASE), jnp.float32, -3.140625, 3.140625), -3.140625, 3.140625),
        "pulse_shift": with_ends(jax.random.randint(part_splits[3], (PULSES, BEAM_BASE), -REACH, REACH + 1), jax.random.fold_in(part_splits[3], 1), -REACH, REACH).astype(jnp.int32),
        "kernel_taps": with_ends(jax.random.randint(part_splits[4], (LEVELS, 2, KERNEL, BEAM_ROWS), 0, BEAM_DEV), jax.random.fold_in(part_splits[4], 1), 0, BEAM_DEV - 1).astype(jnp.int32),
        "merge_shift": with_ends(jax.random.randint(part_splits[5], (LEVELS, 2, BEAM_ROWS), -REACH, REACH + 1), jax.random.fold_in(part_splits[5], 1), -REACH, REACH).astype(jnp.int32),
        "kernel_weights": noise(part_splits[6], (2, LEVELS, 2, KERNEL, BEAM_ROWS), (4 * KERNEL) ** -0.5, 1.0, ((4, 8),), jnp.float32),
    }


def compress(echoes, chirp):
    row_ids = jnp.arange(BINS, dtype=jnp.int32)[:, None]
    col_ids = jnp.arange(BINS, dtype=jnp.int32)[None, :]
    lag_bins = row_ids - col_ids
    inside = (lag_bins >= 0) & (lag_bins < TAPS)
    tap_index = jnp.clip(lag_bins, 0, TAPS - 1)
    real_tap = jnp.where(inside, chirp[0][tap_index], jnp.zeros((), chirp.dtype))
    imag_tap = jnp.where(inside, chirp[1][tap_index], jnp.zeros((), chirp.dtype))
    real_out = jnp.dot(echoes[0], real_tap, preferred_element_type=jnp.float32) + jnp.dot(echoes[1], imag_tap, preferred_element_type=jnp.float32)
    imag_out = jnp.dot(echoes[1], real_tap, preferred_element_type=jnp.float32) - jnp.dot(echoes[0], imag_tap, preferred_element_type=jnp.float32)
    return jnp.stack([real_out, imag_out]).astype(jnp.bfloat16)

def backproject(compressed, pulse_phase, pulse_shift):
    scale = 1.0 / math.sqrt(PULSE_SUB)
    real_w = (jnp.cos(pulse_phase) * scale).astype(jnp.bfloat16)
    imag_w = (jnp.sin(pulse_phase) * scale).astype(jnp.bfloat16)
    padded = jnp.pad(compressed, ((0, 0), (0, 0), (REACH, REACH)))

    def one_block(block):
        start = (block * PULSE_SUB).astype(jnp.int32)
        data_block = lax.dynamic_slice_in_dim(padded, start, PULSE_SUB, 1)
        real_block = lax.dynamic_slice_in_dim(real_w, start, PULSE_SUB, 0)
        imag_block = lax.dynamic_slice_in_dim(imag_w, start, PULSE_SUB, 0)
        shift_block = lax.dynamic_slice_in_dim(pulse_shift, start, PULSE_SUB, 0)
        zero_value = jnp.zeros((), real_block.dtype)
        summed_re = jnp.zeros((BEAM_BASE, BINS), jnp.float32)
        summed_im = jnp.zeros((BEAM_BASE, BINS), jnp.float32)
        for offset in range(-REACH, REACH + 1):
            matches = shift_block == offset
            real_q = jnp.where(matches, real_block, zero_value).T
            imag_q = jnp.where(matches, imag_block, zero_value).T
            window = data_block[:, :, REACH + offset:REACH + offset + BINS]
            summed_re = summed_re + jnp.dot(real_q, window[0], preferred_element_type=jnp.float32) - jnp.dot(imag_q, window[1], preferred_element_type=jnp.float32)
            summed_im = summed_im + jnp.dot(real_q, window[1], preferred_element_type=jnp.float32) + jnp.dot(imag_q, window[0], preferred_element_type=jnp.float32)
        return jnp.stack([summed_re, summed_im]).astype(jnp.bfloat16)
    blocks = lax.map(one_block, jnp.arange(N_APER, dtype=jnp.int32))
    return blocks.transpose(1, 0, 2, 3).reshape(2, BEAM_ROWS, BINS)

def merge_level(image, level, kernel_taps, merge_shift, kernel_weights):
    block_count = BEAM_ROWS // BEAM_DEV
    child_blocks = BEAM_BASE * 2 ** level // BEAM_DEV
    block_ids = np.arange(block_count)
    base_ids = block_ids - child_blocks * (block_ids // child_blocks % 2)
    blocks = image.reshape(2, block_count, BEAM_DEV, BINS)
    beam_ids = jnp.arange(BEAM_DEV, dtype=jnp.int32)
    summed_re = jnp.zeros((block_count, BEAM_DEV, BINS), jnp.float32)
    summed_im = jnp.zeros((block_count, BEAM_DEV, BINS), jnp.float32)
    for child_index in range(2):
        source = blocks[:, base_ids + child_index * child_blocks].astype(jnp.float32)
        source = jnp.pad(source, ((0, 0), (0, 0), (0, 0), (REACH, REACH)))
        matches = kernel_taps[level, child_index][:, :, None] == beam_ids[None, None, :]
        real_k = lax.optimization_barrier(jnp.sum(jnp.where(matches, kernel_weights[0, level, child_index][:, :, None], 0.0), axis=0)).astype(jnp.bfloat16)
        imag_k = lax.optimization_barrier(jnp.sum(jnp.where(matches, kernel_weights[1, level, child_index][:, :, None], 0.0), axis=0)).astype(jnp.bfloat16)
        shifts = merge_shift[level, child_index][:, None]
        zero_value = jnp.zeros((), real_k.dtype)
        for offset in range(-REACH, REACH + 1):
            chosen = shifts == offset
            real_sel = jnp.where(chosen, real_k, zero_value).astype(jnp.float32).reshape(block_count, BEAM_DEV, BEAM_DEV)
            imag_sel = jnp.where(chosen, imag_k, zero_value).astype(jnp.float32).reshape(block_count, BEAM_DEV, BEAM_DEV)
            window = source[..., REACH + offset:REACH + offset + BINS]
            summed_re = summed_re + jnp.einsum('kij,kjr->kir', real_sel, window[0]) - jnp.einsum('kij,kjr->kir', imag_sel, window[1])
            summed_im = summed_im + jnp.einsum('kij,kjr->kir', real_sel, window[1]) + jnp.einsum('kij,kjr->kir', imag_sel, window[0])
    merged = jnp.stack([summed_re, summed_im]).astype(jnp.bfloat16)
    return merged.reshape(2, BEAM_ROWS, BINS)

def reference(echoes, chirp, pulse_phase, pulse_shift, kernel_taps, merge_shift, kernel_weights):
    compressed = compress(echoes, chirp)
    image = backproject(compressed, pulse_phase, pulse_shift)
    for level in range(LEVELS):
        image = merge_level(image, level, kernel_taps, merge_shift, kernel_weights)
    return image
```

```python
import math

import jax
import jax.numpy as jnp
from jax import lax
from jax.experimental import pallas as pl
from jax.experimental.pallas import tpu as pltpu
from jax.sharding import PartitionSpec as P

REACH = 8
BEAM_DEV = 32
PULSE_SUB = 128
LANES = 128
BLOCK = 256
F32 = jnp.float32
BF16 = jnp.bfloat16


def edge_mask(shape, slab):
    lane = lax.broadcasted_iota(jnp.int32, shape, 1)
    index = lax.axis_index("rng")
    last = lax.axis_size("rng") - 1
    right = jnp.where(index < last, 1, 0)
    left = jnp.where(index > 0, 1, 0)
    return jnp.where(lane < LANES // 2, right, left) > 0


def prepare_body(chirp, phase, shift, taps, mshift, mweight, toep, own, send, mats, rows, g_sc, m_sc, s_sc):
    tap_count = chirp.shape[1]
    span = toep.shape[1]
    for part in range(2):
        base = jnp.concatenate(
            [chirp[part : part + 1, :].astype(F32), jnp.zeros((1, span - tap_count), F32)], axis=1
        )
        skewed = pltpu.roll(jnp.broadcast_to(base, (BLOCK, span)), 0, 1, stride=1, stride_axis=0)
        toep[part] = skewed.T.astype(BF16)
    scale = 1.0 / math.sqrt(PULSE_SUB)
    angle = phase[...]
    real = jnp.cos(angle) * scale
    imag = jnp.sin(angle) * scale
    beams = angle.shape[1]
    top = jnp.concatenate([real, -imag], axis=0).T
    bottom = jnp.concatenate([imag, real], axis=0).T
    steps = shift[...].astype(F32)
    steps = jnp.concatenate([steps, steps], axis=0).T
    for half in range(beams // BEAM_DEV):
        at = slice(half * BEAM_DEV, (half + 1) * BEAM_DEV)
        g_sc[half] = jnp.concatenate([top[at], bottom[at], steps[at]], axis=0).astype(BF16)
    sub = lax.axis_index("sub")
    own[...] = g_sc[sub]
    send[...] = g_sc[1 - sub]
    aper = lax.axis_index("aper")
    beam = lax.broadcasted_iota(jnp.int32, (BEAM_DEV, 2 * BEAM_DEV), 0)
    for level in range(taps.shape[0]):
        for child in range(2):
            real_t = jnp.zeros((BEAM_DEV, 2 * BEAM_DEV), F32)
            imag_t = jnp.zeros((BEAM_DEV, 2 * BEAM_DEV), F32)
            tap = taps[level, child]
            tap = jnp.concatenate([tap, tap], axis=1)
            wr = mweight[0, level, child]
            wi = mweight[1, level, child]
            wre = jnp.concatenate([wr, wi], axis=1)
            wim = jnp.concatenate([-wi, wr], axis=1)
            for t in range(tap.shape[0]):
                hit = beam == tap[t : t + 1]
                real_t = real_t + jnp.where(hit, wre[t : t + 1], 0.0)
                imag_t = imag_t + jnp.where(hit, wim[t : t + 1], 0.0)
            m_sc[child] = jnp.concatenate([real_t, imag_t], axis=0).T.astype(BF16)
            step = mshift[level, child : child + 1].astype(F32)
            step = jnp.concatenate([step, step], axis=1)
            s_sc[child] = jnp.broadcast_to(step, (LANES, 2 * BEAM_DEV)).T.astype(jnp.int32)
        side = (aper >> level) & 1
        mats[level, 0] = m_sc[side]
        mats[level, 1] = m_sc[1 - side]
        rows[level, 0] = s_sc[side]
        rows[level, 1] = s_sc[1 - side]


def compress_body(echoes, right, left, toep, out):
    _, count, slab = echoes.shape
    span = toep.shape[1]
    reach = right.shape[2]
    index = lax.axis_index("rng")
    inner = echoes[...].reshape(2 * count, slab)
    right_on = jnp.where(index < lax.axis_size("rng") - 1, 1.0, 0.0).astype(BF16)
    left_on = jnp.where(index > 0, 1.0, 0.0).astype(BF16)
    after = right[...].reshape(2 * count, reach) * right_on
    before = left[:, :, left.shape[2] - LANES :].reshape(2 * count, LANES) * left_on
    ext = jnp.concatenate([inner, after], axis=1)
    blocks = slab // BLOCK
    stacked = jnp.concatenate(
        [ext[:, j * BLOCK : j * BLOCK + span] for j in range(blocks)], axis=0
    )
    by_real = jnp.dot(stacked, toep[0], preferred_element_type=F32)
    by_imag = jnp.dot(stacked, toep[1], preferred_element_type=F32)
    for j in range(blocks):
        a = slice(2 * count * j, 2 * count * j + count)
        b = slice(2 * count * j + count, 2 * count * (j + 1))
        at = slice(j * BLOCK, (j + 1) * BLOCK)
        out[:count, at] = (by_real[a] + by_imag[b]).astype(BF16)
        out[count:, at] = (by_real[b] - by_imag[a]).astype(BF16)
    need = span - BLOCK + LANES
    ends = jnp.concatenate(
        [
            ext[:, slab : slab + need],
            jnp.concatenate([before, ext[:, : need - LANES]], axis=1),
        ],
        axis=0,
    )
    by_real = jnp.dot(ends, toep[0, :need, :LANES], preferred_element_type=F32)
    by_imag = jnp.dot(ends, toep[1, :need, :LANES], preferred_element_type=F32)
    margins = []
    for side in range(2):
        a = slice(2 * count * side, 2 * count * side + count)
        b = slice(2 * count * side + count, 2 * count * (side + 1))
        margins.append(
            jnp.concatenate([by_real[a] + by_imag[b], by_real[b] - by_imag[a]], axis=0)
        )
    shape = margins[0].shape
    lane = lax.broadcasted_iota(jnp.int32, shape, 1)
    margin = jnp.where(lane < LANES // 2, margins[0], margins[1])
    out[:, slab:] = jnp.where(edge_mask(shape, slab), margin, 0.0).astype(BF16)


def project_body(own, other, mine, theirs, out, w_sc, y_sc):
    rows = 2 * BEAM_DEV
    width = out.shape[1]
    weight = jnp.concatenate([own[:rows, :], other[:rows, :]], axis=1)
    step = jnp.concatenate([own[rows:, :], other[rows:, :]], axis=1)
    step = jnp.concatenate([step, step], axis=0)
    offsets = range(-REACH, REACH + 1)
    for k, offset in enumerate(offsets):
        w_sc[k * rows : (k + 1) * rows, :] = jnp.where(
            step == jnp.asarray(offset, BF16), weight, jnp.zeros((), BF16)
        )
    pulses = jnp.concatenate([mine[...], theirs[...]], axis=0)
    y_sc[...] = jnp.dot(w_sc[...], pulses, preferred_element_type=F32)
    total = jnp.zeros((rows, width), F32)
    for k, offset in enumerate(offsets):
        part = y_sc[k * rows : (k + 1) * rows, :]
        total = total + (pltpu.roll(part, (-offset) % width, 1) if offset else part)
    slab = width - LANES
    out[:, :slab] = total[:, :slab].astype(BF16)
    margin = total[:, slab:]
    out[:, slab:] = jnp.where(edge_mask(margin.shape, slab), margin, 0.0).astype(BF16)


def shifted_rows(product, step):
    count = product.shape[1] // LANES
    lane = lax.broadcasted_iota(jnp.int32, step.shape, 1) + step
    index = lane & (LANES - 1)
    over = lane >= LANES
    under = lane < 0
    turned = [
        jnp.take_along_axis(product[:, i * LANES : (i + 1) * LANES], index, axis=1)
        for i in range(count)
    ]
    return [
        jnp.where(
            over, turned[(i + 1) % count], jnp.where(under, turned[(i - 1) % count], turned[i])
        )
        for i in range(count)
    ]


def merge_own_body(child, mats, rows, out, *, level):
    product = jnp.dot(mats[level, 0], child[...], preferred_element_type=F32)
    for i, tile in enumerate(shifted_rows(product, rows[level, 0])):
        out[:, i * LANES : (i + 1) * LANES] = tile


def merge_other_body(child, mats, rows, partial, out, *, level, last):
    product = jnp.dot(mats[level, 1], child[...], preferred_element_type=F32)
    tiles = shifted_rows(product, rows[level, 1])
    slab = child.shape[1] - LANES
    for i, tile in enumerate(tiles):
        at = slice(i * LANES, (i + 1) * LANES)
        value = partial[:, at] + tile
        if last:
            if i * LANES < slab:
                out[0, :, at] = value[:BEAM_DEV].astype(BF16)
                out[1, :, at] = value[BEAM_DEV:].astype(BF16)
        else:
            if i * LANES >= slab:
                value = jnp.where(edge_mask(value.shape, slab), value, 0.0)
            out[:, at] = value.astype(BF16)


def struct(shape, dtype):
    return jax.ShapeDtypeStruct(shape, dtype)


def neighbours(echoes, reach):
    slab = echoes.shape[2]
    size = lax.axis_size("rng")
    if size == 2 and slab >= reach:
        start = jnp.where(lax.axis_index("rng") == 0, slab - reach, 0)
        piece = lax.dynamic_slice_in_dim(echoes, start, reach, 2)
        got = lax.ppermute(piece, "rng", [(0, 1), (1, 0)])
        return got, got
    pieces = []
    distance = 1
    have = 0
    while have < reach:
        take = min(slab, reach - have)
        pairs = [(i, i - distance) for i in range(distance, size)]
        pieces.append(lax.ppermute(echoes[:, :, :take], "rng", pairs))
        have += take
        distance += 1
    pairs = [(i, i + 1) for i in range(size - 1)]
    left = lax.ppermute(echoes[:, :, slab - LANES :], "rng", pairs)
    return jnp.concatenate(pieces, axis=2), left


def shards(echoes, chirp, pulse_phase, pulse_shift, kernel_taps, merge_shift, kernel_weights):
    _, count, slab = echoes.shape
    tap_count = chirp.shape[1]
    levels = kernel_taps.shape[0]
    width = slab + LANES
    rows = 2 * BEAM_DEV
    span = tap_count + BLOCK
    right, left = neighbours(echoes, tap_count + LANES)
    table = (3 * BEAM_DEV, 2 * count)
    toep, own, send, mats, steps = pl.pallas_call(
        prepare_body,
        out_shape=(
            struct((2, span, BLOCK), BF16),
            struct(table, BF16),
            struct(table, BF16),
            struct((levels, 2, rows, rows), BF16),
            struct((levels, 2, rows, LANES), jnp.int32),
        ),
        scratch_shapes=[
            pltpu.VMEM((pulse_phase.shape[1] // BEAM_DEV,) + table, BF16),
            pltpu.VMEM((2, rows, rows), BF16),
            pltpu.VMEM((2, rows, LANES), jnp.int32),
        ],
        name="prepare",
    )(chirp, pulse_phase, pulse_shift, kernel_taps, merge_shift, kernel_weights)
    swap = [(0, 1), (1, 0)]
    other = lax.ppermute(send, "sub", swap)
    mine = pl.pallas_call(
        compress_body, out_shape=struct((2 * count, width), BF16), name="compress"
    )(echoes, right, left, toep)
    theirs = lax.ppermute(mine, "sub", swap)
    offsets = 2 * REACH + 1
    image = pl.pallas_call(
        project_body,
        out_shape=struct((rows, width), BF16),
        scratch_shapes=[
            pltpu.VMEM((offsets * rows, 4 * count), BF16),
            pltpu.VMEM((offsets * rows, width), F32),
        ],
        name="project",
    )(own, other, mine, theirs)
    size = lax.axis_size("aper")
    for level in range(levels):
        last = level == levels - 1
        pairs = [(i, i ^ (1 << level)) for i in range(size)]
        sibling = lax.ppermute(image, "aper", pairs)
        partial = pl.pallas_call(
            lambda *refs, level=level: merge_own_body(*refs, level=level),
            out_shape=struct((rows, width), F32),
            name="merge_own",
        )(image, mats, steps)
        image = pl.pallas_call(
            lambda *refs, level=level, last=last: merge_other_body(*refs, level=level, last=last),
            out_shape=struct((2, BEAM_DEV, slab) if last else (rows, width), BF16),
            name="merge_other",
        )(sibling, mats, steps, partial)
    return image


def solution(mesh):
    placed = (
        P(None, ("parts", "aper", "sub"), "rng"),
        P(),
        P(("parts", "aper", "sub"), None),
        P(("parts", "aper", "sub"), None),
        P(None, None, None, ("parts", "aper", "sub")),
        P(None, None, ("parts", "aper", "sub")),
        P(None, None, None, None, ("parts", "aper", "sub")),
    )
    return jax.shard_map(
        shards,
        mesh=mesh,
        in_specs=placed,
        out_specs=P(None, ("parts", "aper", "sub"), "rng"),
        check_vma=False,
    )
```

```python
import functools
import math

import jax
import jax.numpy as jnp
from jax import lax
from jax.experimental import pallas as pl
from jax.experimental.pallas import tpu as pltpu
from jax.sharding import PartitionSpec as P

REACH = 8
BEAM_DEV = 32
PULSE_SUB = 128
LANES = 128
BLOCK = 256
F32 = jnp.float32
BF16 = jnp.bfloat16


def edge_mask(shape, slab):
    lane = lax.broadcasted_iota(jnp.int32, shape, 1)
    index = lax.axis_index("rng")
    last = lax.axis_size("rng") - 1
    right = jnp.where(index < last, 1, 0)
    left = jnp.where(index > 0, 1, 0)
    return jnp.where(lane < LANES // 2, right, left) > 0


def prepare_body(chirp, phase, shift, taps, mshift, mweight, toep, own, send, mats, rows, g_sc, m_sc, s_sc):
    tap_count = chirp.shape[1]
    span = toep.shape[1]
    for part in range(2):
        base = jnp.concatenate(
            [chirp[part : part + 1, :].astype(F32), jnp.zeros((1, span - tap_count), F32)], axis=1
        )
        skewed = pltpu.roll(jnp.broadcast_to(base, (BLOCK, span)), 0, 1, stride=1, stride_axis=0)
        toep[part] = skewed.T.astype(BF16)
    scale = 1.0 / math.sqrt(PULSE_SUB)
    angle = phase[...]
    real = jnp.cos(angle) * scale
    imag = jnp.sin(angle) * scale
    beams = angle.shape[1]
    top = jnp.concatenate([real, -imag], axis=0).T
    bottom = jnp.concatenate([imag, real], axis=0).T
    steps = shift[...].astype(F32)
    steps = jnp.concatenate([steps, steps], axis=0).T
    for half in range(beams // BEAM_DEV):
        at = slice(half * BEAM_DEV, (half + 1) * BEAM_DEV)
        g_sc[half] = jnp.concatenate([top[at], bottom[at], steps[at]], axis=0).astype(BF16)
    sub = lax.axis_index("sub")
    own[...] = g_sc[sub]
    send[...] = g_sc[1 - sub]
    aper = lax.axis_index("aper")
    beam = lax.broadcasted_iota(jnp.int32, (BEAM_DEV, 2 * BEAM_DEV), 0)
    for level in range(taps.shape[0]):
        for child in range(2):
            real_t = jnp.zeros((BEAM_DEV, 2 * BEAM_DEV), F32)
            imag_t = jnp.zeros((BEAM_DEV, 2 * BEAM_DEV), F32)
            tap = taps[level, child]
            tap = jnp.concatenate([tap, tap], axis=1)
            wr = mweight[0, level, child]
            wi = mweight[1, level, child]
            wre = jnp.concatenate([wr, wi], axis=1)
            wim = jnp.concatenate([-wi, wr], axis=1)
            for t in range(tap.shape[0]):
                hit = beam == tap[t : t + 1]
                real_t = real_t + jnp.where(hit, wre[t : t + 1], 0.0)
                imag_t = imag_t + jnp.where(hit, wim[t : t + 1], 0.0)
            m_sc[child] = jnp.concatenate([real_t, imag_t], axis=0).T.astype(BF16)
            step = mshift[level, child : child + 1].astype(F32)
            step = jnp.concatenate([step, step], axis=1)
            s_sc[child] = jnp.broadcast_to(step, (LANES, 2 * BEAM_DEV)).T.astype(jnp.int32)
        side = (aper >> level) & 1
        mats[level, 0] = m_sc[side]
        mats[level, 1] = m_sc[1 - side]
        rows[level, 0] = s_sc[side]
        rows[level, 1] = s_sc[1 - side]


def compress_body(echoes, right, left, toep, out):
    _, count, slab = echoes.shape
    span = toep.shape[1]
    reach = right.shape[2]
    index = lax.axis_index("rng")
    inner = echoes[...].reshape(2 * count, slab)
    right_on = jnp.where(index < lax.axis_size("rng") - 1, 1.0, 0.0).astype(BF16)
    left_on = jnp.where(index > 0, 1.0, 0.0).astype(BF16)
    after = right[...].reshape(2 * count, reach) * right_on
    before = left[:, :, left.shape[2] - LANES :].reshape(2 * count, LANES) * left_on
    ext = jnp.concatenate([inner, after], axis=1)
    blocks = slab // BLOCK
    stacked = jnp.concatenate(
        [ext[:, j * BLOCK : j * BLOCK + span] for j in range(blocks)], axis=0
    )
    by_real = jnp.dot(stacked, toep[0], preferred_element_type=F32)
    by_imag = jnp.dot(stacked, toep[1], preferred_element_type=F32)
    for j in range(blocks):
        a = slice(2 * count * j, 2 * count * j + count)
        b = slice(2 * count * j + count, 2 * count * (j + 1))
        at = slice(j * BLOCK, (j + 1) * BLOCK)
        out[:count, at] = (by_real[a] + by_imag[b]).astype(BF16)
        out[count:, at] = (by_real[b] - by_imag[a]).astype(BF16)
    need = span - BLOCK + LANES
    ends = jnp.concatenate(
        [
            ext[:, slab : slab + need],
            jnp.concatenate([before, ext[:, : need - LANES]], axis=1),
        ],
        axis=0,
    )
    by_real = jnp.dot(ends, toep[0, :need, :LANES], preferred_element_type=F32)
    by_imag = jnp.dot(ends, toep[1, :need, :LANES], preferred_element_type=F32)
    margins = []
    for side in range(2):
        a = slice(2 * count * side, 2 * count * side + count)
        b = slice(2 * count * side + count, 2 * count * (side + 1))
        margins.append(
            jnp.concatenate([by_real[a] + by_imag[b], by_real[b] - by_imag[a]], axis=0)
        )
    shape = margins[0].shape
    lane = lax.broadcasted_iota(jnp.int32, shape, 1)
    margin = jnp.where(lane < LANES // 2, margins[0], margins[1])
    out[:, slab:] = jnp.where(edge_mask(shape, slab), margin, 0.0).astype(BF16)


def project_body(own, other, mine, theirs, out, w_sc, y_sc):
    rows = 2 * BEAM_DEV
    width = out.shape[1]
    weight = jnp.concatenate([own[:rows, :], other[:rows, :]], axis=1)
    step = jnp.concatenate([own[rows:, :], other[rows:, :]], axis=1)
    step = jnp.concatenate([step, step], axis=0)
    offsets = range(-REACH, REACH + 1)
    for k, offset in enumerate(offsets):
        w_sc[k * rows : (k + 1) * rows, :] = jnp.where(
            step == jnp.asarray(offset, BF16), weight, jnp.zeros((), BF16)
        )
    pulses = jnp.concatenate([mine[...], theirs[...]], axis=0)
    y_sc[...] = jnp.dot(w_sc[...], pulses, preferred_element_type=F32)
    total = jnp.zeros((rows, width), F32)
    for k, offset in enumerate(offsets):
        part = y_sc[k * rows : (k + 1) * rows, :]
        total = total + (pltpu.roll(part, (-offset) % width, 1) if offset else part)
    slab = width - LANES
    out[:, :slab] = total[:, :slab].astype(BF16)
    margin = total[:, slab:]
    out[:, slab:] = jnp.where(edge_mask(margin.shape, slab), margin, 0.0).astype(BF16)


def shifted_rows(product, step):
    count = product.shape[1] // LANES
    lane = lax.broadcasted_iota(jnp.int32, step.shape, 1) + step
    index = lane & (LANES - 1)
    over = lane >= LANES
    under = lane < 0
    turned = [
        jnp.take_along_axis(product[:, i * LANES : (i + 1) * LANES], index, axis=1)
        for i in range(count)
    ]
    return [
        jnp.where(
            over, turned[(i + 1) % count], jnp.where(under, turned[(i - 1) % count], turned[i])
        )
        for i in range(count)
    ]


def merge_own_body(child, mats, rows, out, *, level):
    product = jnp.dot(mats[level, 0], child[...], preferred_element_type=F32)
    for i, tile in enumerate(shifted_rows(product, rows[level, 0])):
        out[:, i * LANES : (i + 1) * LANES] = tile


def merge_other_body(child, mats, rows, partial, out, *, level, last):
    product = jnp.dot(mats[level, 1], child[...], preferred_element_type=F32)
    tiles = shifted_rows(product, rows[level, 1])
    slab = child.shape[1] - LANES
    for i, tile in enumerate(tiles):
        at = slice(i * LANES, (i + 1) * LANES)
        value = partial[:, at] + tile
        if last:
            if i * LANES < slab:
                out[0, :, at] = value[:BEAM_DEV].astype(BF16)
                out[1, :, at] = value[BEAM_DEV:].astype(BF16)
        else:
            if i * LANES >= slab:
                value = jnp.where(edge_mask(value.shape, slab), value, 0.0)
            out[:, at] = value.astype(BF16)


def struct(shape, dtype):
    return jax.ShapeDtypeStruct(shape, dtype)


def local_call(body, args, out_shape, name, limit, scratch=()):
    vmem = pl.BlockSpec(memory_space=pltpu.VMEM)
    return pl.pallas_call(
        body,
        out_shape=out_shape,
        in_specs=[vmem] * len(args),
        out_specs=jax.tree.map(lambda _: vmem, out_shape),
        scratch_shapes=list(scratch),
        compiler_params=pltpu.CompilerParams(vmem_limit_bytes=limit),
        name=name,
    )(*args)


def neighbours(echoes, reach):
    slab = echoes.shape[2]
    size = lax.axis_size("rng")
    if size == 2 and slab >= reach:
        start = jnp.where(lax.axis_index("rng") == 0, slab - reach, 0)
        piece = lax.dynamic_slice_in_dim(echoes, start, reach, 2)
        got = lax.ppermute(piece, "rng", [(0, 1), (1, 0)])
        return got, got
    pieces = []
    distance = 1
    have = 0
    while have < reach:
        take = min(slab, reach - have)
        pairs = [(i, i - distance) for i in range(distance, size)]
        pieces.append(lax.ppermute(echoes[:, :, :take], "rng", pairs))
        have += take
        distance += 1
    pairs = [(i, i + 1) for i in range(size - 1)]
    left = lax.ppermute(echoes[:, :, slab - LANES :], "rng", pairs)
    return jnp.concatenate(pieces, axis=2), left


def shards(echoes, chirp, pulse_phase, pulse_shift, kernel_taps, merge_shift, kernel_weights):
    _, count, slab = echoes.shape
    tap_count = chirp.shape[1]
    levels = kernel_taps.shape[0]
    width = slab + LANES
    rows = 2 * BEAM_DEV
    span = tap_count + BLOCK
    right, left = neighbours(echoes, tap_count + LANES)
    table = (3 * BEAM_DEV, 2 * count)
    toep, own, send, mats, steps = local_call(
        prepare_body,
        (chirp, pulse_phase, pulse_shift, kernel_taps, merge_shift, kernel_weights),
        (
            struct((2, span, BLOCK), BF16),
            struct(table, BF16),
            struct(table, BF16),
            struct((levels, 2, rows, rows), BF16),
            struct((levels, 2, rows, LANES), jnp.int32),
        ),
        "prepare",
        8 << 20,
        (
            pltpu.VMEM((pulse_phase.shape[1] // BEAM_DEV,) + table, BF16),
            pltpu.VMEM((2, rows, rows), BF16),
            pltpu.VMEM((2, rows, LANES), jnp.int32),
        ),
    )
    swap = [(0, 1), (1, 0)]
    other = lax.ppermute(send, "sub", swap)
    mine = local_call(
        compress_body,
        (echoes, right, left, toep),
        struct((2 * count, width), BF16),
        "compress",
        16 << 20,
    )
    theirs = lax.ppermute(mine, "sub", swap)
    offsets = 2 * REACH + 1
    image = local_call(
        project_body,
        (own, other, mine, theirs),
        struct((rows, width), BF16),
        "project",
        16 << 20,
        (
            pltpu.VMEM((offsets * rows, 4 * count), BF16),
            pltpu.VMEM((offsets * rows, width), F32),
        ),
    )
    size = lax.axis_size("aper")
    for level in range(levels):
        last = level == levels - 1
        pairs = [(i, i ^ (1 << level)) for i in range(size)]
        sibling = lax.ppermute(image, "aper", pairs)
        partial = local_call(
            functools.partial(merge_own_body, level=level),
            (image, mats, steps),
            struct((rows, width), F32),
            "merge_own",
            4 << 20,
        )
        image = local_call(
            functools.partial(merge_other_body, level=level, last=last),
            (sibling, mats, steps, partial),
            struct((2, BEAM_DEV, slab) if last else (rows, width), BF16),
            "merge_other",
            4 << 20,
        )
    return image


def solution(mesh):
    placed = (
        P(None, ("parts", "aper", "sub"), "rng"),
        P(),
        P(("parts", "aper", "sub"), None),
        P(("parts", "aper", "sub"), None),
        P(None, None, None, ("parts", "aper", "sub")),
        P(None, None, ("parts", "aper", "sub")),
        P(None, None, None, None, ("parts", "aper", "sub")),
    )
    return jax.shard_map(
        shards,
        mesh=mesh,
        in_specs=placed,
        out_specs=P(None, ("parts", "aper", "sub"), "rng"),
        check_vma=False,
    )
```
